32 devices in a mesh: groups: 2 (over y), vox: 4 (over z), freq: 2 (over x), sub: 2 (over core).
Axes of the slice: x: 2, y: 2, z: 4, core: 2. Of those that a mesh axis runs over, the one named last changes fastest.
Arguments:
- residual: bfloat16 [4, 1024, 1024], P(('groups', 'freq'), 'vox', 'sub'), parts along dimension 0, may hold values from -6 to 6
- green: bfloat16 [4, 1024, 8192], P(('groups', 'freq'), None, 'vox'), parts along dimension 0, may hold values from -0.15625 to 0.15625
- active: int32 [4, 1024], P(('groups', 'freq')), parts along dimension 0, may hold values 0 or 1
- aperture: int32 [4], P(('groups', 'freq')), parts along dimension 0, may hold values from 256 to 511
- step_gain: float32 [4], P(('groups', 'freq')), parts along dimension 0, may hold values from 6 to 24
- block_region: int32 [128], P(('groups', 'vox')), parts along dimension 0, may hold values from 0 to 15
- strength: float32 [16], replicated, may hold values from 0.1 to 1
Outputs:
- updated: float32 [4, 1024, 1024], P(('groups', 'freq'), 'vox', 'sub'), parts along dimension 0
The draws below stay inside these ranges and needn't reach their ends.
There are 2 independent parts, one for each index of `groups`. The reference program is written for one: setup_inputs(seed, part) draws one part's arguments, and reference() takes and returns one part's arrays. A program takes and returns all parts, laid end to end along the dimension named above; an argument that names none is the same for every part. Nothing has to cross between parts.
All inputs are finite; a program needn't handle non-finite values. No bound on the sum of `active` on one device may be relied on, other than what follows from the above.
Results may differ from the reference program's by a relative error of at most 0.0026.
Values may be sent and summed in bfloat16 or wider, within the bound.
A program may use at most 64 MiB of HBM per device.

```python
import math
import jax
import jax.numpy as jnp
from jax import lax

NE = 1024
BLOCK = 128
REGIONS = 16
FREQS = 2
VOXELS = 8192
NBLK = 64


def place_ends(result, own_key, low, high):
    longest = result.shape.index(max(result.shape))
    spots = []
    for shift in (0, 1):
        where = [jax.random.randint(jax.random.fold_in(own_key, axis), (), 0, length) for axis, length in enumerate(result.shape)]
        where[longest] = (where[longest] + shift) % result.shape[longest]
        spots.append(tuple(where))
    return result.at[spots[0]].set(low).at[spots[1]].set(high)


def strengthened(values, rng, source, target, shards_of, factor):
    def block_of(position):
        return (jnp.arange(values.shape[position]) // (values.shape[position] // shards_of)).reshape((-1,) + (1,) * (values.ndim - 1 - position))

    one_side = jax.random.permutation(rng, shards_of)[block_of(target)]
    other_side = (block_of(target) + shards_of // 2) % shards_of
    return jnp.where((block_of(source) == one_side) | (block_of(source) == other_side), factor * values, values)


def block_levels(own_key, shape, pieces, low, largest):
    def one(dim, blocks):
        steps = jax.random.uniform(jax.random.fold_in(jax.random.fold_in(own_key, 6), dim), (blocks,), jnp.float32, low / len(pieces), largest / len(pieces))
        return jnp.repeat(jnp.exp(steps), shape[dim] // blocks).reshape((-1,) + (1,) * (len(shape) - dim - 1))

    loudness = one(*pieces[0])
    for cut in pieces[1:]:
        loudness = loudness * one(*cut)
    return loudness


def normal_values(key, extent, width, bound, split=(), kind=jnp.bfloat16):
    drawn = jax.random.normal(key, extent, jnp.float32) * width
    if len(split) > 0:
        drawn = block_levels(key, extent, split, -0.22, 0.18) * drawn
    return jnp.clip(drawn, min=-bound, max=bound).astype(kind)


def heavy_noise(stream_key, extent, scale, most, cuts, heavy, kind=jnp.bfloat16):
    array = scale * jax.random.normal(stream_key, extent, jnp.float32)
    if cuts:
        array = array * block_levels(stream_key, extent, cuts, -0.22, 0.18)
    return jnp.clip(strengthened(array, jax.random.fold_in(stream_key, 3), *heavy), -most, most).astype(kind)


def setup_inputs(seed: int = 0, part: int = 0) -> dict:
    arg_keys = jax.random.split(jax.random.key(seed), 8)
    own_keys = jax.random.split(jax.random.fold_in(arg_keys[7], part), 8)
    return {
        "residual": normal_values(own_keys[0], (FREQS, NE, NE), 1.0, 6.0, ((0, 2), (1, 4), (2, 2))),
        "green": heavy_noise(own_keys[1], (FREQS, NE, VOXELS), (3 * NE) ** -0.5, 0.15625, ((0, 2), (2, 4)), (2, 1, 4, 2.0)),
        "active": place_ends((jax.random.randint(own_keys[2], (FREQS, NE), 0, 8) < 7).astype(jnp.int32), jax.random.fold_in(own_keys[2], 1), 0, 1),
        "aperture": jax.random.randint(own_keys[3], (FREQS,), NE // 4, NE // 2).astype(jnp.int32),
        "step_gain": jnp.clip(jnp.exp(math.log(24.0) - 1.3862944 * jax.random.uniform(own_keys[4], (FREQS,), jnp.float32) ** block_levels(own_keys[4], (FREQS,), ((0, 2),), -0.2, 0.2)), 6.0, 24.0),
        "block_region": place_ends(jax.random.randint(own_keys[5], (NBLK,), 0, REGIONS), jax.random.fold_in(own_keys[5], 1), 0, REGIONS - 1).astype(jnp.int32),
        "strength": jnp.clip(jnp.exp(jax.random.uniform(arg_keys[6], (REGIONS,), jnp.float32, math.log(0.1), math.log(1.0))), 0.1, 1.0),
    }


smooth_sq = 0.0625

def build_mask(active, aperture):
    element_ids = jnp.arange(NE, dtype=jnp.int32)
    distance = jnp.abs(element_ids[:, None] - element_ids[None, :])
    in_band = (distance[None, :, :] <= aperture[:, None, None]).astype(jnp.int32)
    return active[:, :, None] * active[:, None, :] * in_band

def penalize(image_sum, strength_map):
    return image_sum - strength_map * image_sum / jnp.sqrt(image_sum * image_sum + smooth_sq)

def reference(residual, green, active, aperture, step_gain, block_region, strength):
    pair_mask = build_mask(active, aperture)
    masked = residual * pair_mask.astype(jnp.bfloat16)

    def image_one(operands):
        masked_f, green_f = operands
        beamed = jnp.dot(masked_f.T, green_f, preferred_element_type=jnp.float32)
        return lax.optimization_barrier(jnp.sum(green_f.astype(jnp.float32) * beamed, axis=0))
    image_sum = lax.optimization_barrier(jnp.sum(lax.map(image_one, (masked, green)), axis=0))
    strength_map = jnp.repeat(strength[block_region], BLOCK)
    scaled = penalize(image_sum, strength_map)

    def gradient_one(green_f):
        weighted = (green_f.astype(jnp.float32) * scaled[None, :]).astype(jnp.bfloat16)
        return jnp.dot(green_f, weighted.T, preferred_element_type=jnp.float32)
    gradient = lax.map(gradient_one, green)
    return pair_mask.astype(jnp.float32) * (residual.astype(jnp.float32) - step_gain[:, None, None] * gradient)
```

```python
import jax
import jax.numpy as jnp
from jax import lax
from jax.experimental import pallas as pl
from jax.experimental.pallas import tpu as pltpu
from jax.sharding import PartitionSpec as P

BLOCK = 128
LANES = 128
APERTURE_MAX = 511
smooth_sq = 0.0625
MESH = pl.DeviceIdType.MESH


def penalize(image_sum, strength_map):
    return image_sum - strength_map * image_sum / jnp.sqrt(image_sum * image_sum + smooth_sq)


def make_kernel(n, nf, ns, rows, cols, ne, vox_local, n_blocks):
    tile = min(rows, LANES)
    per = rows // tile
    col_tiles = cols // LANES
    vchunk = min(512, vox_local)
    peers = nf * ns

    def kernel(
        res, green, active, aperture, gain, region, strength, out,
        allm, gv, act_col, mm, img, ar_send, ar_land, wgt, gacc, send_buf, land_r, land_l,
        sem_g, sem_own, agr_s, agr_r, agl_s, agl_r, ar_s, ar_r, rsr_s, rsr_r, rsl_s, rsl_r,
    ):
        z = lax.axis_index("vox")
        f = lax.axis_index("freq")
        s = lax.axis_index("sub")
        has_up = z < n - 1
        has_down = z > 0
        up = {"vox": jnp.minimum(z + 1, n - 1)}
        down = {"vox": jnp.maximum(z - 1, 0)}

        def row_of(block):
            return pl.multiple_of(block * rows, rows)

        own_copy = pltpu.make_async_copy(res, allm.at[pl.ds(row_of(z), rows), :], sem_own)
        own_copy.start()
        green_copy = pltpu.make_async_copy(green, gv, sem_g)
        green_copy.start()

        def peer(k):
            df, ds = k // ns, k % ns
            return {"freq": lax.rem(f + df, nf), "sub": lax.rem(s + ds, ns)}

        barrier = pltpu.get_barrier_semaphore()
        for k in range(1, peers):
            pl.semaphore_signal(barrier, inc=1, device_id=peer(k), device_id_type=MESH)

        @pl.when(has_up)
        def _():
            pl.semaphore_signal(barrier, inc=1, device_id=up, device_id_type=MESH)

        @pl.when(has_down)
        def _():
            pl.semaphore_signal(barrier, inc=1, device_id=down, device_id_type=MESH)

        pl.semaphore_wait(barrier, peers - 1 + has_up.astype(jnp.int32) + has_down.astype(jnp.int32))

        def band(q):
            r0 = q * tile
            first = jnp.int32(0)
            count = jnp.int32(0)
            for j in range(col_tiles):
                c0 = s * cols + j * LANES
                below = c0 + LANES - 1 + APERTURE_MAX < r0
                above = c0 > r0 + tile - 1 + APERTURE_MAX
                first = first + below.astype(jnp.int32)
                count = count + 1 - below.astype(jnp.int32) - above.astype(jnp.int32)
            return first, count

        def per_width(q, fn):
            first, count = band(q)
            for w in range(1, col_tiles + 1):
                @pl.when(count == w)
                def _(w=w):
                    fn(pl.ds(pl.multiple_of(first * LANES, LANES), w * LANES))

        def tile_rows(q):
            return pl.ds(pl.multiple_of(q * tile, tile), tile)

        def remote(src, dst, send, recv, target):
            return pltpu.make_async_remote_copy(
                src_ref=src, dst_ref=dst, send_sem=send, recv_sem=recv,
                device_id=target, device_id_type=MESH,
            )

        def gather_up(q, c):
            a = allm.at[tile_rows(q), c]
            return remote(a, a, agr_s.at[q], agr_r.at[q], up)

        def gather_down(q, c):
            a = allm.at[tile_rows(q), c]
            return remote(a, a, agl_s.at[q], agl_r.at[q], down)

        for t in range(per):
            q = z * per + t

            def first_up(c, q=q, t=t):
                remote(res.at[pl.ds(t * tile, tile), c], allm.at[tile_rows(q), c],
                       agr_s.at[q], agr_r.at[q], up).start()

            def first_down(c, q=q, t=t):
                remote(res.at[pl.ds(t * tile, tile), c], allm.at[tile_rows(q), c],
                       agl_s.at[q], agl_r.at[q], down).start()

            @pl.when(has_up)
            def _():
                per_width(q, first_up)

            @pl.when(has_down)
            def _():
                per_width(q, first_down)

        for i in range(ne // LANES):
            line = active[0:1, i * LANES:(i + 1) * LANES].astype(jnp.float32)
            act_col[i * LANES:(i + 1) * LANES, :] = jnp.broadcast_to(line, (LANES, LANES)).T
        img[...] = jnp.zeros_like(img)
        col0 = pl.multiple_of(s * cols, cols)

        def pair_mask(block):
            r0 = row_of(block)
            rr = lax.broadcasted_iota(jnp.int32, (rows, cols), 0) + r0
            cc = lax.broadcasted_iota(jnp.int32, (rows, cols), 1) + col0
            in_band = jnp.abs(rr - cc) <= aperture[0]
            row_on = act_col[pl.ds(r0, rows), 0:1] > 0.5
            col_on = active[0:1, pl.ds(col0, cols)] > 0
            return in_band & row_on & col_on

        def image_part(block):
            r0 = row_of(block)
            value = allm[pl.ds(r0, rows), :].astype(jnp.float32)
            mm[...] = jnp.where(pair_mask(block), value, 0.0).astype(jnp.bfloat16)

            @pl.loop(0, vox_local // vchunk)
            def _(v):
                vs = pl.ds(pl.multiple_of(v * vchunk, vchunk), vchunk)
                y = jnp.dot(mm[...], gv[pl.ds(col0, cols), vs], preferred_element_type=jnp.float32)
                y = y * gv[pl.ds(r0, rows), vs].astype(jnp.float32)
                img[:, vs] += jnp.sum(y.reshape(rows // 8, 8, vchunk), axis=0)

        own_copy.wait()
        green_copy.wait()
        image_part(z)

        @pl.loop(0, n - 1)
        def _(step):
            from_below = z - 1 - step
            from_above = z + 1 + step
            for t in range(per):
                @pl.when(from_below >= 0)
                def _():
                    q = from_below * per + t

                    def land(c):
                        gather_up(q, c).wait_recv()

                        @pl.when(has_up)
                        def _():
                            gather_up(q, c).start()
                    per_width(q, land)

                @pl.when(from_above < n)
                def _():
                    q = from_above * per + t

                    def land(c):
                        gather_down(q, c).wait_recv()

                        @pl.when(has_down)
                        def _():
                            gather_down(q, c).start()
                    per_width(q, land)

            @pl.when(from_below >= 0)
            def _():
                image_part(from_below)

            @pl.when(from_above < n)
            def _():
                image_part(from_above)

        ar_send[...] = jnp.sum(img[...], axis=0, keepdims=True)
        exchanges = [
            remote(ar_send, ar_land.at[k], ar_s.at[k], ar_r.at[k], peer(k)) for k in range(1, peers)
        ]
        for e in exchanges:
            e.start()
        strength_map = jnp.concatenate(
            [jnp.full((1, BLOCK), strength[region[b]], jnp.float32) for b in range(n_blocks)], axis=1
        )
        for e in exchanges:
            e.wait_recv()
        total = ar_send[...]
        for k in range(1, peers):
            total = total + ar_land[k]
        img[0:1, :] = penalize(total, strength_map)

        wrows = 32

        @pl.loop(0, cols // wrows)
        def _(i):
            src = pl.ds(pl.multiple_of(col0 + i * wrows, wrows), wrows)
            dst = pl.ds(pl.multiple_of(i * wrows, wrows), wrows)
            wgt[dst, :] = (gv[src, :].astype(jnp.float32) * img[0:1, :]).astype(jnp.bfloat16)

        def scatter_up(q, c):
            return remote(send_buf.at[tile_rows(q), c], land_r.at[tile_rows(q), c],
                          rsr_s.at[q], rsr_r.at[q], up)

        def scatter_down(q, c):
            return remote(send_buf.at[tile_rows(q), c], land_l.at[tile_rows(q), c],
                          rsl_s.at[q], rsl_r.at[q], down)

        def each_tile(block, make, act):
            for t in range(per):
                q = block * per + t
                per_width(q, lambda c, q=q: act(make(q, c)))

        def partial_step(k, ends):
            lo, hi = ends
            use_hi = (hi > z) & ((lo >= z) | (z + (n - 1 - hi) <= (n - 1 - z) + lo))
            d = jnp.where(use_hi, hi, lo)
            rs = pl.ds(row_of(d), rows)
            part = lax.dot_general(
                gv[rs, :], wgt[...], (((1,), (1,)), ((), ())), preferred_element_type=jnp.float32
            )
            gacc[rs, :] = part
            sends_up = (d > z) & jnp.logical_not(has_down)
            sends_down = (d < z) & jnp.logical_not(has_up)

            @pl.when(sends_up | sends_down)
            def _():
                send_buf[rs, :] = part.astype(jnp.bfloat16)

            @pl.when(sends_up)
            def _():
                each_tile(d, scatter_up, lambda c: c.start())

            @pl.when(sends_down)
            def _():
                each_tile(d, scatter_down, lambda c: c.start())

            step_hi = use_hi.astype(jnp.int32)
            return lo + 1 - step_hi, hi - step_hi

        lax.fori_loop(0, n, partial_step, (jnp.int32(0), jnp.int32(n - 1)))

        @pl.loop(0, n - 1)
        def _(slot):
            @pl.when(has_down & (slot >= z))
            def _():
                d = z + n - 1 - slot
                for t in range(per):
                    q = d * per + t

                    def add(c):
                        scatter_up(q, c).wait_recv()
                        send_buf[tile_rows(q), c] = (
                            gacc[tile_rows(q), c] + land_r[tile_rows(q), c].astype(jnp.float32)
                        ).astype(jnp.bfloat16)
                        scatter_up(q, c).start()
                    per_width(q, add)

            @pl.when(has_up & (slot >= n - 1 - z))
            def _():
                d = slot - (n - 1 - z)
                for t in range(per):
                    q = d * per + t

                    def add(c):
                        scatter_down(q, c).wait_recv()
                        send_buf[tile_rows(q), c] = (
                            gacc[tile_rows(q), c] + land_l[tile_rows(q), c].astype(jnp.float32)
                        ).astype(jnp.bfloat16)
                        scatter_down(q, c).start()
                    per_width(q, add)

        @pl.when(has_down)
        def _():
            each_tile(z, scatter_up, lambda c: c.wait_recv())

        @pl.when(has_up)
        def _():
            each_tile(z, scatter_down, lambda c: c.wait_recv())

        mine = pl.ds(row_of(z), rows)
        gradient = gacc[mine, :]
        gradient = gradient + jnp.where(has_down, land_r[mine, :].astype(jnp.float32), 0.0)
        gradient = gradient + jnp.where(has_up, land_l[mine, :].astype(jnp.float32), 0.0)
        data = allm[mine, :].astype(jnp.float32)
        out[...] = jnp.where(pair_mask(z), data - gain[0] * gradient, 0.0)

        for e in exchanges:
            e.wait_send()

        @pl.loop(0, n)
        def _(b):
            @pl.when(has_up & (b <= z))
            def _():
                each_tile(b, gather_up, lambda c: c.wait_send())

            @pl.when(has_down & (b >= z))
            def _():
                each_tile(b, gather_down, lambda c: c.wait_send())

            @pl.when(has_up & (b > z))
            def _():
                each_tile(b, scatter_up, lambda c: c.wait_send())

            @pl.when(has_down & (b < z))
            def _():
                each_tile(b, scatter_down, lambda c: c.wait_send())

    tiles = n * per
    dma = pltpu.SemaphoreType.DMA
    scratch = [
        pltpu.VMEM((ne, cols), jnp.bfloat16),
        pltpu.VMEM((ne, vox_local), jnp.bfloat16),
        pltpu.VMEM((ne, LANES), jnp.float32),
        pltpu.VMEM((rows, cols), jnp.bfloat16),
        pltpu.VMEM((8, vox_local), jnp.float32),
        pltpu.VMEM((1, vox_local), jnp.float32),
        pltpu.VMEM((peers, 1, vox_local), jnp.float32),
        pltpu.VMEM((cols, vox_local), jnp.bfloat16),
        pltpu.VMEM((ne, cols), jnp.float32),
        pltpu.VMEM((ne, cols), jnp.bfloat16),
        pltpu.VMEM((ne, cols), jnp.bfloat16),
        pltpu.VMEM((ne, cols), jnp.bfloat16),
        dma, dma,
        dma((tiles,)), dma((tiles,)), dma((tiles,)), dma((tiles,)),
        dma((peers,)), dma((peers,)),
        dma((tiles,)), dma((tiles,)), dma((tiles,)), dma((tiles,)),
    ]
    return kernel, scratch


def solution(mesh):
    sizes = dict(mesh.shape)

    def body(residual, green, active, aperture, step_gain, block_region, strength):
        _, rows, cols = residual.shape
        _, ne, vox_local = green.shape
        kernel, scratch = make_kernel(
            sizes["vox"], sizes["freq"], sizes["sub"], rows, cols, ne, vox_local,
            block_region.shape[0],
        )
        vmem = pl.BlockSpec(memory_space=pltpu.VMEM)
        smem = pl.BlockSpec(memory_space=pltpu.SMEM)
        any_space = pl.BlockSpec(memory_space=pl.ANY)
        updated = pl.pallas_call(
            kernel,
            out_shape=jax.ShapeDtypeStruct((rows, cols), jnp.float32),
            in_specs=[any_space, any_space, vmem, smem, smem, smem, smem],
            out_specs=vmem,
            scratch_shapes=scratch,
            compiler_params=pltpu.CompilerParams(
                collective_id=0, has_side_effects=True, vmem_limit_bytes=48 * 1024 * 1024
            ),
            name="imaging_step",
        )(residual[0], green[0], active, aperture, step_gain, block_region, strength)
        return updated[None]

    in_specs = (
        P(("groups", "freq"), "vox", "sub"),
        P(("groups", "freq"), None, "vox"),
        P(("groups", "freq"), None),
        P(("groups", "freq")),
        P(("groups", "freq")),
        P(("groups", "vox")),
        P(),
    )
    out_specs = P(("groups", "freq"), "vox", "sub")
    return jax.shard_map(body, mesh=mesh, in_specs=in_specs, out_specs=out_specs, check_vma=False)
```

```python
import jax
import jax.numpy as jnp
from jax import lax
from jax.experimental import pallas as pl
from jax.experimental.pallas import tpu as pltpu
from jax.sharding import PartitionSpec as P

BLOCK = 128
LANES = 128
APERTURE_MAX = 511
smooth_sq = 0.0625
FULL, UP, DOWN = range(3)
MESH = pl.DeviceIdType.MESH


def penalize(image_sum, strength_map):
    return image_sum - strength_map * image_sum / jnp.sqrt(image_sum * image_sum + smooth_sq)


def make_kernel(n, nf, ns, rows, cols, ne, vox_local, n_blocks, regions):
    tile = min(rows, LANES)
    per = rows // tile
    col_tiles = cols // LANES
    vchunk = min(512, vox_local)
    peers = nf * ns

    def kernel(
        res, green, active_in, aperture_in, gain_in, region_in, strength_in, out,
        active, aperture, gain, region, strength, sem_small,
        allm, gv, act_col, mm, img, ar_send, ar_land, wgt, gacc, flipped, send_buf, land_r, land_l,
        sem_g, sem_own, agr_s, agr_r, agl_s, agl_r, ar_s, ar_r, rsr_s, rsr_r, rsl_s, rsl_r,
    ):
        z = lax.axis_index("vox")
        f = lax.axis_index("freq")
        s = lax.axis_index("sub")
        has_up = z < n - 1
        has_down = z > 0
        up = {"vox": jnp.minimum(z + 1, n - 1)}
        down = {"vox": jnp.maximum(z - 1, 0)}

        def row_of(block):
            return pl.multiple_of(block * rows, rows)

        small = [
            pltpu.make_async_copy(a, b, sem_small.at[i])
            for i, (a, b) in enumerate((
                (active_in, active), (aperture_in, aperture), (gain_in, gain),
                (region_in, region), (strength_in, strength),
            ))
        ]
        for c in small:
            c.start()
        own_copy = pltpu.make_async_copy(res, allm.at[pl.ds(row_of(z), rows), :], sem_own)
        own_copy.start()
        green_copy = pltpu.make_async_copy(green, gv, sem_g)
        green_copy.start()

        def peer(k):
            df, ds = k // ns, k % ns
            return {"freq": lax.rem(f + df, nf), "sub": lax.rem(s + ds, ns)}

        barrier = pltpu.get_barrier_semaphore()
        for k in range(1, peers):
            pl.semaphore_signal(barrier, inc=1, device_id=peer(k), device_id_type=MESH)

        @pl.when(has_up)
        def _():
            pl.semaphore_signal(barrier, inc=1, device_id=up, device_id_type=MESH)

        @pl.when(has_down)
        def _():
            pl.semaphore_signal(barrier, inc=1, device_id=down, device_id_type=MESH)

        pl.semaphore_wait(barrier, peers - 1 + has_up.astype(jnp.int32) + has_down.astype(jnp.int32))

        def square(q):
            local = q * tile - s * cols
            inside = (local >= 0) & (local < cols)
            return inside, jnp.clip(local, 0, cols - 1) // LANES

        def band(q, kind):
            r0 = q * tile
            inside, diag = square(q)
            first = jnp.int32(0)
            count = jnp.int32(0)
            for j in range(col_tiles):
                c0 = s * cols + j * LANES
                below = c0 + LANES - 1 + APERTURE_MAX < r0
                above = c0 > r0 + tile - 1 + APERTURE_MAX
                if kind == UP:
                    above = above | (inside & (j > diag))
                if kind == DOWN:
                    below = below | (inside & (j < diag))
                first = first + below.astype(jnp.int32)
                count = count + 1 - below.astype(jnp.int32) - above.astype(jnp.int32)
            return first, count

        def per_width(q, fn, kind=FULL):
            first, count = band(q, kind)
            for w in range(1, col_tiles + 1):
                @pl.when(count == w)
                def _(w=w):
                    fn(pl.ds(pl.multiple_of(first * LANES, LANES), w * LANES))

        def tile_rows(q):
            return pl.ds(pl.multiple_of(q * tile, tile), tile)

        def remote(src, dst, send, recv, target):
            return pltpu.make_async_remote_copy(
                src_ref=src, dst_ref=dst, send_sem=send, recv_sem=recv,
                device_id=target, device_id_type=MESH,
            )

        def gather_up(q, c):
            a = allm.at[tile_rows(q), c]
            return remote(a, a, agr_s.at[q], agr_r.at[q], up)

        def gather_down(q, c):
            a = allm.at[tile_rows(q), c]
            return remote(a, a, agl_s.at[q], agl_r.at[q], down)

        for t in range(per):
            q = z * per + t

            def first_up(c, q=q, t=t):
                remote(res.at[pl.ds(t * tile, tile), c], allm.at[tile_rows(q), c],
                       agr_s.at[q], agr_r.at[q], up).start()

            def first_down(c, q=q, t=t):
                remote(res.at[pl.ds(t * tile, tile), c], allm.at[tile_rows(q), c],
                       agl_s.at[q], agl_r.at[q], down).start()

            @pl.when(has_up)
            def _():
                per_width(q, first_up)

            @pl.when(has_down)
            def _():
                per_width(q, first_down)

        for c in small:
            c.wait()
        for i in range(ne // LANES):
            line = active[0:1, i * LANES:(i + 1) * LANES].astype(jnp.float32)
            act_col[i * LANES:(i + 1) * LANES, :] = jnp.broadcast_to(line, (LANES, LANES)).T
        img[...] = jnp.zeros_like(img)
        col0 = pl.multiple_of(s * cols, cols)

        def pair_mask(block):
            r0 = row_of(block)
            rr = lax.broadcasted_iota(jnp.int32, (rows, cols), 0) + r0
            cc = lax.broadcasted_iota(jnp.int32, (rows, cols), 1) + col0
            in_band = jnp.abs(rr - cc) <= aperture[0]
            row_on = act_col[pl.ds(r0, rows), 0:1] > 0.5
            col_on = active[0:1, pl.ds(col0, cols)] > 0
            return in_band & row_on & col_on

        def image_part(block):
            r0 = row_of(block)
            value = allm[pl.ds(r0, rows), :].astype(jnp.float32)
            mm[...] = jnp.where(pair_mask(block), value, 0.0).astype(jnp.bfloat16)

            @pl.loop(0, vox_local // vchunk)
            def _(v):
                vs = pl.ds(pl.multiple_of(v * vchunk, vchunk), vchunk)
                y = jnp.dot(mm[...], gv[pl.ds(col0, cols), vs], preferred_element_type=jnp.float32)
                y = y * gv[pl.ds(r0, rows), vs].astype(jnp.float32)
                img[:, vs] += jnp.sum(y.reshape(rows // 8, 8, vchunk), axis=0)

        own_copy.wait()
        green_copy.wait()
        image_part(z)

        @pl.loop(0, n - 1)
        def _(step):
            from_below = z - 1 - step
            from_above = z + 1 + step
            for t in range(per):
                @pl.when(from_below >= 0)
                def _():
                    q = from_below * per + t

                    def land(c):
                        gather_up(q, c).wait_recv()

                        @pl.when(has_up)
                        def _():
                            gather_up(q, c).start()
                    per_width(q, land)

                @pl.when(from_above < n)
                def _():
                    q = from_above * per + t

                    def land(c):
                        gather_down(q, c).wait_recv()

                        @pl.when(has_down)
                        def _():
                            gather_down(q, c).start()
                    per_width(q, land)

            @pl.when(from_below >= 0)
            def _():
                image_part(from_below)

            @pl.when(from_above < n)
            def _():
                image_part(from_above)

        ar_send[...] = jnp.sum(img[...], axis=0, keepdims=True)
        exchanges = [
            remote(ar_send, ar_land.at[k], ar_s.at[k], ar_r.at[k], peer(k)) for k in range(1, peers)
        ]
        for e in exchanges:
            e.start()
        strength_map = jnp.concatenate(
            [jnp.full((1, BLOCK), strength[region[b]], jnp.float32) for b in range(n_blocks)], axis=1
        )
        for e in exchanges:
            e.wait_recv()
        total = ar_send[...]
        for k in range(1, peers):
            total = total + ar_land[k]
        img[0:1, :] = penalize(total, strength_map)

        wrows = 32

        @pl.loop(0, cols // wrows)
        def _(i):
            src = pl.ds(pl.multiple_of(col0 + i * wrows, wrows), wrows)
            dst = pl.ds(pl.multiple_of(i * wrows, wrows), wrows)
            wgt[dst, :] = (gv[src, :].astype(jnp.float32) * img[0:1, :]).astype(jnp.bfloat16)

        def scatter_up(q, c):
            return remote(send_buf.at[tile_rows(q), c], land_r.at[tile_rows(q), c],
                          rsr_s.at[q], rsr_r.at[q], up)

        def scatter_down(q, c):
            return remote(send_buf.at[tile_rows(q), c], land_l.at[tile_rows(q), c],
                          rsl_s.at[q], rsl_r.at[q], down)

        def each_tile(block, make, act, kind=FULL):
            for t in range(per):
                q = block * per + t
                per_width(q, lambda c, q=q: act(make(q, c)), kind)

        def partial_step(k, ends):
            lo, hi = ends
            use_hi = (hi > z) & ((lo >= z) | (z + (n - 1 - hi) <= (n - 1 - z) + lo))
            d = jnp.where(use_hi, hi, lo)
            rs = pl.ds(row_of(d), rows)
            part = lax.dot_general(
                gv[rs, :], wgt[...], (((1,), (1,)), ((), ())), preferred_element_type=jnp.float32
            )
            gacc[rs, :] = part
            sends_up = (d > z) & jnp.logical_not(has_down)
            sends_down = (d < z) & jnp.logical_not(has_up)

            @pl.when(sends_up | sends_down)
            def _():
                send_buf[rs, :] = part.astype(jnp.bfloat16)

            @pl.when(sends_up)
            def _():
                each_tile(d, scatter_up, lambda c: c.start(), UP)

            @pl.when(sends_down)
            def _():
                each_tile(d, scatter_down, lambda c: c.start(), DOWN)

            step_hi = use_hi.astype(jnp.int32)
            return lo + 1 - step_hi, hi - step_hi

        lax.fori_loop(0, n, partial_step, (jnp.int32(0), jnp.int32(n - 1)))

        @pl.loop(0, n - 1)
        def _(slot):
            @pl.when(has_down & (slot >= z))
            def _():
                d = z + n - 1 - slot
                for t in range(per):
                    q = d * per + t

                    def add(c):
                        scatter_up(q, c).wait_recv()
                        send_buf[tile_rows(q), c] = (
                            gacc[tile_rows(q), c] + land_r[tile_rows(q), c].astype(jnp.float32)
                        ).astype(jnp.bfloat16)
                        scatter_up(q, c).start()
                    per_width(q, add, UP)

            @pl.when(has_up & (slot >= n - 1 - z))
            def _():
                d = slot - (n - 1 - z)
                for t in range(per):
                    q = d * per + t

                    def add(c):
                        scatter_down(q, c).wait_recv()
                        send_buf[tile_rows(q), c] = (
                            gacc[tile_rows(q), c] + land_l[tile_rows(q), c].astype(jnp.float32)
                        ).astype(jnp.bfloat16)
                        scatter_down(q, c).start()
                    per_width(q, add, DOWN)

        @pl.when(has_down)
        def _():
            each_tile(z, scatter_up, lambda c: c.wait_recv(), UP)

        @pl.when(has_up)
        def _():
            each_tile(z, scatter_down, lambda c: c.wait_recv(), DOWN)

        mine = pl.ds(row_of(z), rows)
        def add_landed(land, there, q, mirrored):
            inside, diag = square(q)
            offset = lax.rem(q * tile, LANES)
            for j in range(col_tiles):
                c = slice(j * LANES, (j + 1) * LANES)
                flip = inside & mirrored(j, diag)

                @pl.when(there & jnp.logical_not(flip))
                def _():
                    gacc[tile_rows(q), c] += land[tile_rows(q), c].astype(jnp.float32)

                @pl.when(there & flip)
                def _():
                    twin = pl.ds(pl.multiple_of(col0 + j * LANES, LANES), LANES)
                    own = pl.ds(pl.multiple_of(diag * LANES, LANES), LANES)
                    flipped[...] = land[twin, own].astype(jnp.float32).T
                    gacc[tile_rows(q), c] += flipped[pl.ds(pl.multiple_of(offset, tile), tile), :]

        for t in range(per):
            add_landed(land_r, has_down, z * per + t, lambda j, diag: j > diag)
            add_landed(land_l, has_up, z * per + t, lambda j, diag: j < diag)
        gradient = gacc[mine, :]
        data = allm[mine, :].astype(jnp.float32)
        out[...] = jnp.where(pair_mask(z), data - gain[0] * gradient, 0.0)

        for e in exchanges:
            e.wait_send()

        @pl.loop(0, n)
        def _(b):
            @pl.when(has_up & (b <= z))
            def _():
                each_tile(b, gather_up, lambda c: c.wait_send())

            @pl.when(has_down & (b >= z))
            def _():
                each_tile(b, gather_down, lambda c: c.wait_send())

            @pl.when(has_up & (b > z))
            def _():
                each_tile(b, scatter_up, lambda c: c.wait_send(), UP)

            @pl.when(has_down & (b < z))
            def _():
                each_tile(b, scatter_down, lambda c: c.wait_send(), DOWN)

    tiles = n * per
    dma = pltpu.SemaphoreType.DMA
    scratch = [
        pltpu.VMEM((1, ne), jnp.int32),
        pltpu.SMEM((1,), jnp.int32),
        pltpu.SMEM((1,), jnp.float32),
        pltpu.SMEM((n_blocks,), jnp.int32),
        pltpu.SMEM((regions,), jnp.float32),
        dma((5,)),
        pltpu.VMEM((ne, cols), jnp.bfloat16),
        pltpu.VMEM((ne, vox_local), jnp.bfloat16),
        pltpu.VMEM((ne, LANES), jnp.float32),
        pltpu.VMEM((rows, cols), jnp.bfloat16),
        pltpu.VMEM((8, vox_local), jnp.float32),
        pltpu.VMEM((1, vox_local), jnp.float32),
        pltpu.VMEM((peers, 1, vox_local), jnp.float32),
        pltpu.VMEM((cols, vox_local), jnp.bfloat16),
        pltpu.VMEM((ne, cols), jnp.float32),
        pltpu.VMEM((LANES, LANES), jnp.float32),
        pltpu.VMEM((ne, cols), jnp.bfloat16),
        pltpu.VMEM((ne, cols), jnp.bfloat16),
        pltpu.VMEM((ne, cols), jnp.bfloat16),
        dma, dma,
        dma((tiles,)), dma((tiles,)), dma((tiles,)), dma((tiles,)),
        dma((peers,)), dma((peers,)),
        dma((tiles,)), dma((tiles,)), dma((tiles,)), dma((tiles,)),
    ]
    return kernel, scratch


def solution(mesh):
    sizes = dict(mesh.shape)

    def body(residual, green, active, aperture, step_gain, block_region, strength):
        _, rows, cols = residual.shape
        _, ne, vox_local = green.shape
        kernel, scratch = make_kernel(
            sizes["vox"], sizes["freq"], sizes["sub"], rows, cols, ne, vox_local,
            block_region.shape[0], strength.shape[0],
        )
        vmem = pl.BlockSpec(memory_space=pltpu.VMEM)
        hbm = pl.BlockSpec(memory_space=pltpu.HBM)
        updated = pl.pallas_call(
            kernel,
            out_shape=jax.ShapeDtypeStruct((rows, cols), jnp.float32),
            in_specs=[hbm] * 7,
            out_specs=vmem,
            scratch_shapes=scratch,
            compiler_params=pltpu.CompilerParams(
                collective_id=0, has_side_effects=True, vmem_limit_bytes=60 * 1024 * 1024
            ),
            name="imaging_step",
        )(residual[0], green[0], active, aperture, step_gain, block_region, strength)
        return updated[None]

    in_specs = (
        P(("groups", "freq"), "vox", "sub"),
        P(("groups", "freq"), None, "vox"),
        P(("groups", "freq"), None),
        P(("groups", "freq")),
        P(("groups", "freq")),
        P(("groups", "vox")),
        P(),
    )
    out_specs = P(("groups", "freq"), "vox", "sub")
    return jax.shard_map(body, mesh=mesh, in_specs=in_specs, out_specs=out_specs, check_vma=False)
```

```python
import jax
import jax.numpy as jnp
from jax import lax
from jax.experimental import pallas as pl
from jax.experimental.pallas import tpu as pltpu
from jax.sharding import PartitionSpec as P

BLOCK = 128
LANES = 128
APERTURE_MAX = 511
smooth_sq = 0.0625
FULL, UP, DOWN = range(3)
MESH = pl.DeviceIdType.MESH


def penalize(image_sum, strength_map):
    return image_sum - strength_map * image_sum / jnp.sqrt(image_sum * image_sum + smooth_sq)


def make_kernel(n, nf, ns, rows, cols, ne, vox_local, n_blocks, regions):
    tile = min(rows, LANES)
    per = rows // tile
    col_tiles = cols // LANES
    vchunk = min(512, vox_local)
    peers = nf * ns

    def kernel(
        res, green, active_in, aperture_in, gain_in, region_in, strength_in, out,
        active, aperture, gain, region, strength, sem_small,
        allm, gv, act_col, mm, img, ar_send, ar_land, wgt, gacc, flipped, send_buf, land_r, land_l,
        sem_g, sem_own, agr_s, agr_r, agl_s, agl_r, ar_s, ar_r, rsr_s, rsr_r, rsl_s, rsl_r,
    ):
        z = lax.axis_index("vox")
        f = lax.axis_index("freq")
        s = lax.axis_index("sub")
        has_up = z < n - 1
        has_down = z > 0
        up = {"vox": jnp.minimum(z + 1, n - 1)}
        down = {"vox": jnp.maximum(z - 1, 0)}

        def row_of(block):
            return pl.multiple_of(block * rows, rows)

        small = [
            pltpu.make_async_copy(a, b, sem_small.at[i])
            for i, (a, b) in enumerate((
                (active_in, active), (aperture_in, aperture), (gain_in, gain),
                (region_in, region), (strength_in, strength),
            ))
        ]
        for c in small:
            c.start()
        own_copy = pltpu.make_async_copy(res, allm.at[pl.ds(row_of(z), rows), :], sem_own)
        own_copy.start()
        green_copy = pltpu.make_async_copy(green, gv, sem_g)
        green_copy.start()

        def peer(k):
            df, ds = k // ns, k % ns
            return {"freq": lax.rem(f + df, nf), "sub": lax.rem(s + ds, ns)}

        barrier = pltpu.get_barrier_semaphore()
        for k in range(1, peers):
            pl.semaphore_signal(barrier, inc=1, device_id=peer(k), device_id_type=MESH)

        @pl.when(has_up)
        def _():
            pl.semaphore_signal(barrier, inc=1, device_id=up, device_id_type=MESH)

        @pl.when(has_down)
        def _():
            pl.semaphore_signal(barrier, inc=1, device_id=down, device_id_type=MESH)

        pl.semaphore_wait(barrier, peers - 1 + has_up.astype(jnp.int32) + has_down.astype(jnp.int32))

        def square(q):
            local = q * tile - s * cols
            inside = (local >= 0) & (local < cols)
            return inside, lax.div(jnp.clip(local, 0, cols - 1), LANES)

        def band(q, kind):
            reach = q * tile - s * cols + ne
            shift = ne // LANES + APERTURE_MAX // LANES + 1
            lift = LANES * (shift - ne // LANES)
            first = lax.div(reach + lift - APERTURE_MAX, LANES) - shift
            last = lax.div(reach + lift + tile - 1 + APERTURE_MAX, LANES) - shift + 1
            first = jnp.clip(first, 0, col_tiles)
            last = jnp.clip(last, 0, col_tiles)
            if kind != FULL:
                inside, diag = square(q)
            if kind == UP:
                last = jnp.where(inside, jnp.minimum(last, diag + 1), last)
            if kind == DOWN:
                first = jnp.where(inside, jnp.maximum(first, diag), first)
            return first, last - first

        def per_width(q, fn, kind=FULL):
            first, count = band(q, kind)
            for w in range(1, col_tiles + 1):
                @pl.when(count == w)
                def _(w=w):
                    fn(pl.ds(pl.multiple_of(first * LANES, LANES), w * LANES))

        def tile_rows(q):
            return pl.ds(pl.multiple_of(q * tile, tile), tile)

        def remote(src, dst, send, recv, target):
            return pltpu.make_async_remote_copy(
                src_ref=src, dst_ref=dst, send_sem=send, recv_sem=recv,
                device_id=target, device_id_type=MESH,
            )

        def each_tile(block, make, act, kind=FULL):
            for t in range(per):
                q = block * per + t
                per_width(q, lambda c, q=q: act(make(q, c)), kind)

        def gather_up(q, c):
            a = allm.at[tile_rows(q), c]
            return remote(a, a, agr_s.at[q], agr_r.at[q], up)

        def gather_down(q, c):
            a = allm.at[tile_rows(q), c]
            return remote(a, a, agl_s.at[q], agl_r.at[q], down)

        for t in range(per):
            q = z * per + t

            def first_up(c, q=q, t=t):
                remote(res.at[pl.ds(t * tile, tile), c], allm.at[tile_rows(q), c],
                       agr_s.at[q], agr_r.at[q], up).start()

            def first_down(c, q=q, t=t):
                remote(res.at[pl.ds(t * tile, tile), c], allm.at[tile_rows(q), c],
                       agl_s.at[q], agl_r.at[q], down).start()

            @pl.when(has_up)
            def _():
                per_width(q, first_up)

            @pl.when(has_down)
            def _():
                per_width(q, first_down)

        for c in small:
            c.wait()
        for i in range(ne // LANES):
            line = active[0:1, i * LANES:(i + 1) * LANES].astype(jnp.float32)
            act_col[i * LANES:(i + 1) * LANES, :] = jnp.broadcast_to(line, (LANES, LANES)).T
        img[...] = jnp.zeros_like(img)
        col0 = pl.multiple_of(s * cols, cols)

        def pair_mask(block):
            r0 = row_of(block)
            rr = lax.broadcasted_iota(jnp.int32, (rows, cols), 0) + r0
            cc = lax.broadcasted_iota(jnp.int32, (rows, cols), 1) + col0
            in_band = jnp.abs(rr - cc) <= aperture[0]
            row_on = act_col[pl.ds(r0, rows), 0:1] > 0.5
            col_on = active[0:1, pl.ds(col0, cols)] > 0
            return in_band & row_on & col_on

        def image_part(block):
            r0 = row_of(block)
            value = allm[pl.ds(r0, rows), :].astype(jnp.float32)
            mm[...] = jnp.where(pair_mask(block), value, 0.0).astype(jnp.bfloat16)

            @pl.loop(0, vox_local // vchunk)
            def _(v):
                vs = pl.ds(pl.multiple_of(v * vchunk, vchunk), vchunk)
                y = jnp.dot(mm[...], gv[pl.ds(col0, cols), vs], preferred_element_type=jnp.float32)
                y = y * gv[pl.ds(r0, rows), vs].astype(jnp.float32)
                img[:, vs] += jnp.sum(y.reshape(rows // 8, 8, vchunk), axis=0)

        own_copy.wait()
        green_copy.wait()
        image_part(z)

        @pl.loop(0, n - 1)
        def _(step):
            from_below = z - 1 - step
            from_above = z + 1 + step
            for t in range(per):
                @pl.when(from_below >= 0)
                def _():
                    q = from_below * per + t

                    def land(c):
                        gather_up(q, c).wait_recv()

                        @pl.when(has_up)
                        def _():
                            gather_up(q, c).start()
                    per_width(q, land)

                @pl.when(from_above < n)
                def _():
                    q = from_above * per + t

                    def land(c):
                        gather_down(q, c).wait_recv()

                        @pl.when(has_down)
                        def _():
                            gather_down(q, c).start()
                    per_width(q, land)

            @pl.when(from_below >= 0)
            def _():
                image_part(from_below)

            @pl.when(from_above < n)
            def _():
                image_part(from_above)

        ar_send[...] = jnp.sum(img[...], axis=0, keepdims=True)
        exchanges = [
            remote(ar_send, ar_land.at[k], ar_s.at[k], ar_r.at[k], peer(k)) for k in range(1, peers)
        ]
        for e in exchanges:
            e.start()
        strength_map = jnp.concatenate(
            [jnp.full((1, BLOCK), strength[region[b]], jnp.float32) for b in range(n_blocks)], axis=1
        )

        @pl.loop(0, n)
        def _(b):
            @pl.when(has_up & (b <= z))
            def _():
                each_tile(b, gather_up, lambda c: c.wait_send())

            @pl.when(has_down & (b >= z))
            def _():
                each_tile(b, gather_down, lambda c: c.wait_send())

        for e in exchanges:
            e.wait_recv()
        total = ar_send[...]
        for k in range(1, peers):
            total = total + ar_land[k]
        img[0:1, :] = penalize(total, strength_map)

        wrows = 32

        @pl.loop(0, cols // wrows)
        def _(i):
            src = pl.ds(pl.multiple_of(col0 + i * wrows, wrows), wrows)
            dst = pl.ds(pl.multiple_of(i * wrows, wrows), wrows)
            wgt[dst, :] = (gv[src, :].astype(jnp.float32) * img[0:1, :]).astype(jnp.bfloat16)

        def scatter_up(q, c):
            return remote(send_buf.at[tile_rows(q), c], land_r.at[tile_rows(q), c],
                          rsr_s.at[q], rsr_r.at[q], up)

        def scatter_down(q, c):
            return remote(send_buf.at[tile_rows(q), c], land_l.at[tile_rows(q), c],
                          rsl_s.at[q], rsl_r.at[q], down)

        def partial_step(k, ends):
            lo, hi = ends
            use_hi = (hi > z) & ((lo >= z) | (z + (n - 1 - hi) <= (n - 1 - z) + lo))
            d = jnp.where(use_hi, hi, lo)
            rs = pl.ds(row_of(d), rows)
            part = lax.dot_general(
                gv[rs, :], wgt[...], (((1,), (1,)), ((), ())), preferred_element_type=jnp.float32
            )
            gacc[rs, :] = part
            sends_up = (d > z) & jnp.logical_not(has_down)
            sends_down = (d < z) & jnp.logical_not(has_up)

            @pl.when(sends_up | sends_down)
            def _():
                send_buf[rs, :] = part.astype(jnp.bfloat16)

            @pl.when(sends_up)
            def _():
                each_tile(d, scatter_up, lambda c: c.start(), UP)

            @pl.when(sends_down)
            def _():
                each_tile(d, scatter_down, lambda c: c.start(), DOWN)

            step_hi = use_hi.astype(jnp.int32)
            return lo + 1 - step_hi, hi - step_hi

        lax.fori_loop(0, n, partial_step, (jnp.int32(0), jnp.int32(n - 1)))

        @pl.loop(0, n - 1)
        def _(slot):
            @pl.when(has_down & (slot >= z))
            def _():
                d = z + n - 1 - slot
                for t in range(per):
                    q = d * per + t

                    def add(c):
                        scatter_up(q, c).wait_recv()
                        send_buf[tile_rows(q), c] = (
                            gacc[tile_rows(q), c] + land_r[tile_rows(q), c].astype(jnp.float32)
                        ).astype(jnp.bfloat16)
                        scatter_up(q, c).start()
                    per_width(q, add, UP)

            @pl.when(has_up & (slot >= n - 1 - z))
            def _():
                d = slot - (n - 1 - z)
                for t in range(per):
                    q = d * per + t

                    def add(c):
                        scatter_down(q, c).wait_recv()
                        send_buf[tile_rows(q), c] = (
                            gacc[tile_rows(q), c] + land_l[tile_rows(q), c].astype(jnp.float32)
                        ).astype(jnp.bfloat16)
                        scatter_down(q, c).start()
                    per_width(q, add, DOWN)

        @pl.when(has_down)
        def _():
            each_tile(z, scatter_up, lambda c: c.wait_recv(), UP)

        @pl.when(has_up)
        def _():
            each_tile(z, scatter_down, lambda c: c.wait_recv(), DOWN)

        mine = pl.ds(row_of(z), rows)
        def add_landed(land, there, q, mirrored):
            inside, diag = square(q)
            offset = lax.rem(q * tile, LANES)
            for j in range(col_tiles):
                c = slice(j * LANES, (j + 1) * LANES)
                flip = inside & mirrored(j, diag)

                @pl.when(there & jnp.logical_not(flip))
                def _():
                    gacc[tile_rows(q), c] += land[tile_rows(q), c].astype(jnp.float32)

                @pl.when(there & flip)
                def _():
                    twin = pl.ds(pl.multiple_of(col0 + j * LANES, LANES), LANES)
                    own = pl.ds(pl.multiple_of(diag * LANES, LANES), LANES)
                    flipped[...] = land[twin, own].astype(jnp.float32).T
                    gacc[tile_rows(q), c] += flipped[pl.ds(pl.multiple_of(offset, tile), tile), :]

        for t in range(per):
            add_landed(land_r, has_down, z * per + t, lambda j, diag: j > diag)
            add_landed(land_l, has_up, z * per + t, lambda j, diag: j < diag)
        gradient = gacc[mine, :]
        data = allm[mine, :].astype(jnp.float32)
        out[...] = jnp.where(pair_mask(z), data - gain[0] * gradient, 0.0)

        for e in exchanges:
            e.wait_send()

        @pl.loop(0, n)
        def _(b):
            @pl.when(has_up & (b > z))
            def _():
                each_tile(b, scatter_up, lambda c: c.wait_send(), UP)

            @pl.when(has_down & (b < z))
            def _():
                each_tile(b, scatter_down, lambda c: c.wait_send(), DOWN)

    tiles = n * per
    dma = pltpu.SemaphoreType.DMA
    scratch = [
        pltpu.VMEM((1, ne), jnp.int32),
        pltpu.SMEM((1,), jnp.int32),
        pltpu.SMEM((1,), jnp.float32),
        pltpu.SMEM((n_blocks,), jnp.int32),
        pltpu.SMEM((regions,), jnp.float32),
        dma((5,)),
        pltpu.VMEM((ne, cols), jnp.bfloat16),
        pltpu.VMEM((ne, vox_local), jnp.bfloat16),
        pltpu.VMEM((ne, LANES), jnp.float32),
        pltpu.VMEM((rows, cols), jnp.bfloat16),
        pltpu.VMEM((8, vox_local), jnp.float32),
        pltpu.VMEM((1, vox_local), jnp.float32),
        pltpu.VMEM((peers, 1, vox_local), jnp.float32),
        pltpu.VMEM((cols, vox_local), jnp.bfloat16),
        pltpu.VMEM((ne, cols), jnp.float32),
        pltpu.VMEM((LANES, LANES), jnp.float32),
        pltpu.VMEM((ne, cols), jnp.bfloat16),
        pltpu.VMEM((ne, cols), jnp.bfloat16),
        pltpu.VMEM((ne, cols), jnp.bfloat16),
        dma, dma,
        dma((tiles,)), dma((tiles,)), dma((tiles,)), dma((tiles,)),
        dma((peers,)), dma((peers,)),
        dma((tiles,)), dma((tiles,)), dma((tiles,)), dma((tiles,)),
    ]
    return kernel, scratch


def solution(mesh):
    sizes = dict(mesh.shape)

    def body(residual, green, active, aperture, step_gain, block_region, strength):
        _, rows, cols = residual.shape
        _, ne, vox_local = green.shape
        kernel, scratch = make_kernel(
            sizes["vox"], sizes["freq"], sizes["sub"], rows, cols, ne, vox_local,
            block_region.shape[0], strength.shape[0],
        )
        vmem = pl.BlockSpec(memory_space=pltpu.VMEM)
        hbm = pl.BlockSpec(memory_space=pltpu.HBM)
        updated = pl.pallas_call(
            kernel,
            out_shape=jax.ShapeDtypeStruct((rows, cols), jnp.float32),
            in_specs=[hbm] * 7,
            out_specs=vmem,
            scratch_shapes=scratch,
            compiler_params=pltpu.CompilerParams(
                collective_id=0, has_side_effects=True, vmem_limit_bytes=60 * 1024 * 1024
            ),
            name="imaging_step",
        )(residual[0], green[0], active, aperture, step_gain, block_region, strength)
        return updated[None]

    in_specs = (
        P(("groups", "freq"), "vox", "sub"),
        P(("groups", "freq"), None, "vox"),
        P(("groups", "freq"), None),
        P(("groups", "freq")),
        P(("groups", "freq")),
        P(("groups", "vox")),
        P(),
    )
    out_specs = P(("groups", "freq"), "vox", "sub")
    return jax.shard_map(body, mesh=mesh, in_specs=in_specs, out_specs=out_specs, check_vma=False)
```
